32 devices in a mesh: segment: 2 (over y), frame: 16 (over z, x, core).
Axes of the slice: x: 2, y: 2, z: 4, core: 2. Of those that a mesh axis runs over, the one named last changes fastest.
Arguments:
- noisy_clips: bfloat16 [4, 16, 16, 16, 512], P(None, 'frame'), may hold values from -6 to 6
- conv_first: bfloat16 [2, 9, 512, 512], P('segment', None, 'frame'), may hold values from -0.09375 to 0.09375
- conv_second: bfloat16 [2, 9, 512, 512], P('segment', None, 'frame'), may hold values from -0.09375 to 0.09375
- temporal: bfloat16 [2, 3, 512, 512], P('segment', None, 'frame'), may hold values from -0.15625 to 0.15625
Outputs:
- denoised: bfloat16 [4, 16, 16, 16, 512], P(None, 'frame', 'segment')
The draws below stay inside these ranges and needn't reach their ends.
All inputs are finite; a program needn't handle non-finite values.
Results may differ from the reference program's by a relative error of at most 0.013.
Values may be sent and summed in bfloat16 or wider, within the bound.
A program may use at most 64 MiB of HBM per device.

```python
import jax
import jax.numpy as jnp

C = 512
MAP = 16
CLIPS = 4
SECTIONS = 2
FRAMES = 16


def shard_levels(stream_key, shape, split, low, high):
    factor_of = 1.0
    for position, blocks in split:
        steps = jax.random.uniform(jax.random.fold_in(jax.random.fold_in(stream_key, 6), position), (blocks,), jnp.float32, low / len(split), high / len(split))
        factor_of = factor_of * jnp.repeat(jnp.exp(steps), shape[position] // blocks).reshape((-1,) + (1,) * (len(shape) - 1 - position))
    return factor_of


def gaussian(own_key, shape, scale, reach, shards=(), kind=jnp.bfloat16):
    array = scale * jax.random.normal(own_key, shape, jnp.float32)
    if shards:
        array = array * shard_levels(own_key, shape, shards, -0.22, 0.18)
    return jnp.clip(array, -reach, reach).astype(kind)


def setup_inputs(seed: int = 0) -> dict:
    key_list = jax.random.split(jax.random.key(seed), 5)
    return {
        "noisy_clips": gaussian(key_list[0], (CLIPS, FRAMES, MAP, MAP, C), 1.0, 6.0, ((1, 16),)),
        "conv_first": gaussian(key_list[1], (SECTIONS, 9, C, C), (9 * C) ** -0.5, 0.09375, ((0, 2), (2, 16))),
        "conv_second": gaussian(key_list[2], (SECTIONS, 9, C, C), (9 * C) ** -0.5, 0.09375, ((0, 2), (2, 16))),
        "temporal": gaussian(key_list[3], (SECTIONS, 3, C, C), (3 * C) ** -0.5, 0.15625, ((0, 2), (2, 16))),
    }


skip_scale = 0.7071067811865476


def spatial(field_in, kernel):
    extent = field_in.shape[1]
    channels = field_in.shape[3]
    padded = jnp.pad(field_in, ((0, 0), (1, 1), (1, 1), (0, 0)))
    accumulated = jnp.zeros((field_in.shape[0] * extent * extent, channels), jnp.float32)
    for row_shift in range(3):
        for col_shift in range(3):
            window = padded[:, row_shift:row_shift + extent, col_shift:col_shift + extent, :].reshape(-1, channels)
            accumulated = accumulated + jnp.dot(window, kernel[3 * row_shift + col_shift], preferred_element_type=jnp.float32)
    return accumulated.reshape(field_in.shape)


def section(entering, first_kernel, second_kernel, time_kernel):
    full_shape = entering.shape
    channels = full_shape[4]
    frame_total = full_shape[1]
    flat = entering.reshape((-1,) + full_shape[2:])
    activated = jax.nn.silu(spatial(flat, first_kernel)).astype(jnp.bfloat16)
    spatial_term = spatial(activated, second_kernel).reshape(full_shape)
    activated = activated.reshape(full_shape)
    extended = jnp.pad(activated, ((0, 0), (1, 1), (0, 0), (0, 0), (0, 0)))
    time_term = jnp.zeros(full_shape, jnp.float32)
    for offset in range(3):
        window = extended[:, offset:offset + frame_total].reshape(-1, channels)
        time_term = time_term + jnp.dot(window, time_kernel[offset], preferred_element_type=jnp.float32).reshape(full_shape)
    return (entering.astype(jnp.float32) + jax.nn.silu(spatial_term + time_term)).astype(jnp.bfloat16)


def reference(noisy_clips, conv_first, conv_second, temporal):
    sections = conv_first.shape[0]
    half_sections = sections // 2
    current = noisy_clips
    inputs_down = []
    for section_index in range(sections):
        if section_index < half_sections:
            entering = current
            inputs_down.append(current)
        else:
            partner = inputs_down[sections - 1 - section_index]
            entering = ((current.astype(jnp.float32) + partner.astype(jnp.float32)) * skip_scale).astype(jnp.bfloat16)
        current = section(entering, conv_first[section_index], conv_second[section_index], temporal[section_index])
    return current
```

```python
import functools

import jax
import jax.numpy as jnp
from jax import lax
from jax.experimental import pallas as pl
from jax.experimental.pallas import tpu as pltpu
from jax.sharding import PartitionSpec as P

skip_scale = 0.7071067811865476
MESH = pl.DeviceIdType.MESH


def stream_parts(sections, taps):
    parts = max(1, 8 // sections)
    edges = [taps * i // parts for i in range(parts + 1)]
    return [
        (rel, edges[i], edges[i + 1] - edges[i]) for rel in range(sections) for i in range(parts)
    ]


def gather_kernel(
    sections, frames, streams, blk_ref, w_ref, loc_sem, y_send, y_recv, r_send, r_recv, p_send, p_recv
):
    taps, depth = blk_ref.shape[1], blk_ref.shape[2]
    n = frames // 2
    seg = lax.axis_index("segment")
    me = lax.axis_index("frame")
    core, chip = lax.rem(me, 2), me // 2
    other = chip * 2 + (1 - core)

    def chip_at(place):
        return jnp.where(place < n // 2, 2 * place, 2 * (n - 1 - place) + 1)

    pos = jnp.where(lax.rem(chip, 2) == 0, chip // 2, n - 1 - chip // 2)

    def frame_at(place):
        return chip_at(lax.rem(place + 2 * n, n)) * 2 + core

    right, left = frame_at(pos + 1), frame_at(pos - 1)

    barrier = pltpu.get_barrier_semaphore()
    for off in range(1, sections):
        pl.semaphore_signal(
            barrier, inc=1, device_id=(lax.rem(seg + off, sections), me), device_id_type=MESH
        )
    for peer in (right, left, other):
        pl.semaphore_signal(barrier, inc=1, device_id=(seg, peer), device_id_type=MESH)
    pl.semaphore_wait(barrier, sections + 2)

    def rows(owner):
        return pl.ds(pl.multiple_of(owner * depth, depth), depth)

    def y_copy(off):
        peer = lax.rem(seg + off, sections)
        return pltpu.make_async_remote_copy(
            src_ref=blk_ref.at[peer],
            dst_ref=w_ref.at[pl.ds(seg * taps, taps), rows(me)],
            send_sem=y_send.at[off - 1],
            recv_sem=y_recv.at[off - 1],
            device_id=(peer, me),
            device_id_type=MESH,
        )

    local = pltpu.make_async_copy(
        blk_ref.at[seg], w_ref.at[pl.ds(seg * taps, taps), rows(me)], loc_sem
    )
    local.start()
    for off in range(1, sections):
        y_copy(off).start()

    def slab(q, step):
        rel, first, count = streams[q]
        owner = frame_at(pos - step if q % 2 == 0 else pos + step)
        base = lax.rem(seg + sections - rel, sections) * taps + first
        return w_ref.at[pl.ds(base, count), rows(owner)]

    def ring(q, step):
        return pltpu.make_async_remote_copy(
            src_ref=slab(q, step),
            dst_ref=slab(q, step),
            send_sem=r_send.at[q, step],
            recv_sem=r_recv.at[q, step],
            device_id=(seg, right if q % 2 == 0 else left),
            device_id_type=MESH,
        )

    def paired(q, step):
        return pltpu.make_async_remote_copy(
            src_ref=slab(q, step),
            dst_ref=slab(q, step),
            send_sem=p_send.at[q, step],
            recv_sem=p_recv.at[q, step],
            device_id=(seg, other),
            device_id_type=MESH,
        )

    per = len(streams) // sections
    for rel in range(sections):
        if rel == 0:
            local.wait()
        else:
            y_copy(rel).wait_recv()
        for q in range(rel * per, (rel + 1) * per):
            ring(q, 0).start()
            paired(q, 0).start()

    @pl.loop(0, n - 2)
    def _(step):
        for q in range(len(streams)):
            ring(q, step).wait_recv()
            ring(q, step + 1).start()
            paired(q, step + 1).start()

    for q in range(len(streams)):
        ring(q, n - 2).wait_recv()
        paired(q, n - 1).start()

    for off in range(1, sections):
        y_copy(off).wait_send()

    @pl.loop(0, n - 1)
    def _(step):
        for q in range(len(streams)):
            ring(q, step).wait_send()
            paired(q, step).wait()

    for q in range(len(streams)):
        paired(q, n - 1).wait()


def gathered(blocks, sections, frames):
    taps, depth, width = blocks.shape[1:]
    streams = stream_parts(sections, taps)
    count, n = len(streams), frames // 2
    dma = pltpu.SemaphoreType.DMA
    return pl.pallas_call(
        functools.partial(gather_kernel, sections, frames, streams),
        out_shape=jax.ShapeDtypeStruct((sections * taps, frames * depth, width), blocks.dtype),
        in_specs=[pl.BlockSpec(memory_space=pltpu.VMEM)],
        out_specs=pl.BlockSpec(memory_space=pltpu.VMEM),
        scratch_shapes=[
            dma,
            dma((max(sections - 1, 1),)),
            dma((max(sections - 1, 1),)),
            dma((count, n)),
            dma((count, n)),
            dma((count, n)),
            dma((count, n)),
        ],
        compiler_params=pltpu.CompilerParams(
            collective_id=0, has_side_effects=True, vmem_limit_bytes=58 * 1024 * 1024
        ),
    )(blocks)


def conv(field, kernel):
    lead = field.shape[:-3]
    out = lax.conv_general_dilated(
        field.reshape((-1,) + field.shape[-3:]),
        kernel.reshape((3, 3) + kernel.shape[1:]),
        (1, 1),
        "SAME",
        dimension_numbers=("NHWC", "HWIO", "NHWC"),
        preferred_element_type=jnp.float32,
    )
    return out.reshape(lead + out.shape[1:])


def whole_channels(piece, sections, seg):
    if sections == 2:
        theirs = lax.ppermute(piece, "segment", [(0, 1), (1, 0)])
        return jnp.where(
            seg == 0,
            jnp.concatenate([piece, theirs], axis=-1),
            jnp.concatenate([theirs, piece], axis=-1),
        )
    return lax.all_gather(piece, "segment", axis=piece.ndim - 1, tiled=True)


def passed_along(shard, axis, by):
    length = lax.axis_size(axis)
    pairs = [(i, i + by) for i in range(length) if 0 <= i + by < length]
    return lax.ppermute(shard, axis, pairs)


def extended_2(cells, sides, width):
    for axis, dim in sides:
        count = lax.axis_size(axis)
        ends = count - 1
        head = lax.slice_in_dim(cells, 0, width, axis=dim)
        tail = lax.slice_in_dim(cells, cells.shape[dim] - width, cells.shape[dim], axis=dim)
        cells = jnp.concatenate(
            [
                lax.ppermute(tail, axis, [(i, (i + 1) % count) for i in range(ends)]),
                cells,
                lax.ppermute(head, axis, [((i + 1) % count, i) for i in range(ends)]),
            ],
            axis=dim,
        )
    return cells


def broadcast(shard, axis, root):
    mine = lax.axis_index(axis) == root
    return lax.psum(jnp.where(mine, shard, jnp.zeros_like(shard)), axis)


def spatial(field_in, kernel):
    extent = field_in.shape[1]
    channels = field_in.shape[3]
    padded = jnp.pad(field_in, ((0, 0), (1, 1), (1, 1), (0, 0)))
    accumulated = jnp.zeros((field_in.shape[0] * extent * extent, channels), jnp.float32)
    for row_shift in range(3):
        for col_shift in range(3):
            window = padded[
                :, row_shift : row_shift + extent, col_shift : col_shift + extent, :
            ].reshape(-1, channels)
            accumulated = accumulated + jnp.dot(
                window, kernel[3 * row_shift + col_shift], preferred_element_type=jnp.float32
            )
    return accumulated.reshape(field_in.shape)


def temporal_mix(extended, kernel, frame_local):
    channels = extended.shape[3]
    out_shape = (frame_local,) + extended.shape[1:]
    accumulated = jnp.zeros(out_shape, jnp.float32)
    for offset in range(3):
        window = extended[offset : offset + frame_local].reshape(-1, channels)
        accumulated = accumulated + jnp.dot(
            window, kernel[offset], preferred_element_type=jnp.float32
        ).reshape(out_shape)
    return accumulated


def pipelined(noisy_clips, conv_first, conv_second, temporal):
    sections = lax.axis_size("segment")
    segment_id = lax.axis_index("segment")
    first_full, second_full, time_full = (
        lax.all_gather(conv_first, "frame", axis=2, tiled=True),
        lax.all_gather(conv_second, "frame", axis=2, tiled=True),
        lax.all_gather(temporal, "frame", axis=2, tiled=True),
    )
    first_kernel = first_full[0]
    second_kernel = second_full[0]
    time_kernel = time_full[0]
    clip_count = noisy_clips.shape[0]
    frame_local = noisy_clips.shape[1]
    side_len = noisy_clips.shape[2]
    block_shape = noisy_clips.shape[1:]
    tick_count = clip_count + sections - 1
    half_sections = sections // 2
    is_up = segment_id >= half_sections
    store_depth = max(half_sections - 1, 1)
    side_store = jnp.zeros((store_depth,) + block_shape, jnp.bfloat16)
    out_store = jnp.zeros(noisy_clips.shape, jnp.bfloat16)
    prev_out = jnp.zeros(block_shape, jnp.bfloat16)

    def tick_step(carry, tick_index):
        prev_out, side_store, out_store = carry
        clip_now = tick_index - segment_id
        active = (clip_now >= 0) & (clip_now < clip_count)
        clip_slot = jnp.clip(clip_now, 0, clip_count - 1)
        own_input = lax.dynamic_index_in_dim(noisy_clips, clip_slot, 0, keepdims=False)
        received, side_store = passed_along((prev_out, side_store), "segment", 1)
        entering = jnp.where(segment_id == 0, own_input, received)
        written = (jnp.arange(store_depth) == segment_id - 1) & (segment_id < half_sections)
        side_store = jnp.where(written[:, None, None, None, None], entering[None], side_store)
        stack_slot = jnp.clip(sections - 2 - segment_id, 0, store_depth - 1)
        stored = lax.dynamic_index_in_dim(side_store, stack_slot, 0, keepdims=False)
        skip_feature = jnp.where(segment_id == sections - 1, own_input, stored)
        joined = (
            (entering.astype(jnp.float32) + skip_feature.astype(jnp.float32)) * skip_scale
        ).astype(jnp.bfloat16)
        section_in = jnp.where(is_up, joined, entering)
        activated = lax.cond(
            active,
            lambda: jax.nn.silu(spatial(section_in, first_kernel)).astype(jnp.bfloat16),
            lambda: jnp.zeros(block_shape, jnp.bfloat16),
        )
        extended = extended_2(activated, (("frame", 0),), 1)

        def second_pass():
            branch_sum = spatial(activated, second_kernel) + temporal_mix(
                extended, time_kernel, frame_local
            )
            return (section_in.astype(jnp.float32) + jax.nn.silu(branch_sum)).astype(jnp.bfloat16)

        section_out = lax.cond(active, second_pass, lambda: jnp.zeros(block_shape, jnp.bfloat16))
        finished = (jnp.arange(clip_count) == clip_slot) & active & (segment_id == sections - 1)
        out_store = jnp.where(finished[:, None, None, None, None], section_out[None], out_store)
        return ((section_out, side_store, out_store), None)

    final_carry, unused = lax.scan(
        tick_step, (prev_out, side_store, out_store), jnp.arange(tick_count, dtype=jnp.int32)
    )
    delivered = broadcast(final_carry[2], "segment", sections - 1)
    slab_rows = side_len // sections
    return lax.dynamic_slice_in_dim(delivered, segment_id * slab_rows, slab_rows, 2)


def on_device(noisy_clips, conv_first, conv_second, temporal):
    sections = lax.axis_size("segment")
    frames = lax.axis_size("frame")
    seg = lax.axis_index("segment")
    channels = noisy_clips.shape[-1]
    width = channels // sections
    if width % 128 or frames % 4:
        return pipelined(noisy_clips, conv_first, conv_second, temporal)
    stacked = jnp.concatenate([conv_first[0], temporal[0], conv_second[0]], axis=0)
    taps, depth = stacked.shape[0], stacked.shape[1]
    blocks = stacked.reshape(taps, depth, sections, width).transpose(2, 0, 1, 3)
    weights = gathered(blocks, sections, frames)
    forward = [(i, i + 1) for i in range(frames - 1)]
    backward = [(i + 1, i) for i in range(frames - 1)]

    def mine(full):
        return lax.dynamic_slice_in_dim(full, seg * width, width, full.ndim - 1)

    entering = noisy_clips
    entering_mine = mine(noisy_clips)
    down = []
    for s in range(sections):
        part = weights[s * taps : (s + 1) * taps]
        if s < sections // 2:
            down.append(entering_mine)
        active = jax.nn.silu(conv(entering, part[:9])).astype(jnp.bfloat16)
        active = whole_channels(active, sections, seg)

        def mixed(k):
            return jnp.dot(active, part[9 + k], preferred_element_type=jnp.float32)

        after = mixed(0).astype(jnp.bfloat16)
        before = mixed(2).astype(jnp.bfloat16)
        from_prev = lax.ppermute(after[:, -1:], "frame", forward)
        from_next = lax.ppermute(before[:, :1], "frame", backward)
        branch = conv(active, part[12:]) + mixed(1)
        branch = branch + jnp.concatenate([from_prev, after[:, :-1]], axis=1).astype(jnp.float32)
        branch = branch + jnp.concatenate([before[:, 1:], from_next], axis=1).astype(jnp.float32)
        out_mine = (entering_mine.astype(jnp.float32) + jax.nn.silu(branch)).astype(jnp.bfloat16)
        if s + 1 < sections:
            entering_mine = out_mine
            if s + 1 >= sections // 2:
                skip = down[sections - 2 - s]
                entering_mine = (
                    (out_mine.astype(jnp.float32) + skip.astype(jnp.float32)) * skip_scale
                ).astype(jnp.bfloat16)
            entering = whole_channels(entering_mine, sections, seg)
    slab = out_mine.shape[2] // sections
    if sections == 2:
        own = lax.dynamic_slice_in_dim(out_mine, seg * slab, slab, 2)
        away = lax.dynamic_slice_in_dim(out_mine, (1 - seg) * slab, slab, 2)
        theirs = lax.ppermute(away, "segment", [(0, 1), (1, 0)])
        return jnp.where(
            seg == 0,
            jnp.concatenate([own, theirs], axis=-1),
            jnp.concatenate([theirs, own], axis=-1),
        )
    return lax.all_to_all(out_mine, "segment", 2, 4, tiled=True)


def solution(mesh):
    in_specs = (
        P(None, "frame", None, None, None),
        P("segment", None, "frame", None),
        P("segment", None, "frame", None),
        P("segment", None, "frame", None),
    )
    out_specs = P(None, "frame", "segment", None, None)
    return jax.shard_map(
        on_device, mesh=mesh, in_specs=in_specs, out_specs=out_specs, check_vma=False
    )
```

```python
import functools

import jax
import jax.numpy as jnp
from jax import lax
from jax.experimental import pallas as pl
from jax.experimental.pallas import tpu as pltpu
from jax.sharding import PartitionSpec as P

skip_scale = 0.7071067811865476
MESH = pl.DeviceIdType.MESH


def passed_along(shard, axis, by):
    length = lax.axis_size(axis)
    pairs = [(i, i + by) for i in range(length) if 0 <= i + by < length]
    return lax.ppermute(shard, axis, pairs)


def extended_2(cells, sides, width):
    for axis, dim in sides:
        count = lax.axis_size(axis)
        ends = count - 1
        head = lax.slice_in_dim(cells, 0, width, axis=dim)
        tail = lax.slice_in_dim(cells, cells.shape[dim] - width, cells.shape[dim], axis=dim)
        cells = jnp.concatenate(
            [
                lax.ppermute(tail, axis, [(i, (i + 1) % count) for i in range(ends)]),
                cells,
                lax.ppermute(head, axis, [((i + 1) % count, i) for i in range(ends)]),
            ],
            axis=dim,
        )
    return cells


def broadcast(shard, axis, root):
    mine = lax.axis_index(axis) == root
    return lax.psum(jnp.where(mine, shard, jnp.zeros_like(shard)), axis)


def spatial(field_in, kernel):
    extent = field_in.shape[1]
    channels = field_in.shape[3]
    padded = jnp.pad(field_in, ((0, 0), (1, 1), (1, 1), (0, 0)))
    accumulated = jnp.zeros((field_in.shape[0] * extent * extent, channels), jnp.float32)
    for row_shift in range(3):
        for col_shift in range(3):
            window = padded[
                :, row_shift : row_shift + extent, col_shift : col_shift + extent, :
            ].reshape(-1, channels)
            accumulated = accumulated + jnp.dot(
                window, kernel[3 * row_shift + col_shift], preferred_element_type=jnp.float32
            )
    return accumulated.reshape(field_in.shape)


def temporal_mix(extended, kernel, frame_local):
    channels = extended.shape[3]
    out_shape = (frame_local,) + extended.shape[1:]
    accumulated = jnp.zeros(out_shape, jnp.float32)
    for offset in range(3):
        window = extended[offset : offset + frame_local].reshape(-1, channels)
        accumulated = accumulated + jnp.dot(
            window, kernel[offset], preferred_element_type=jnp.float32
        ).reshape(out_shape)
    return accumulated


def pipelined(noisy_clips, conv_first, conv_second, temporal):
    sections = lax.axis_size("segment")
    segment_id = lax.axis_index("segment")
    first_full, second_full, time_full = (
        lax.all_gather(conv_first, "frame", axis=2, tiled=True),
        lax.all_gather(conv_second, "frame", axis=2, tiled=True),
        lax.all_gather(temporal, "frame", axis=2, tiled=True),
    )
    first_kernel = first_full[0]
    second_kernel = second_full[0]
    time_kernel = time_full[0]
    clip_count = noisy_clips.shape[0]
    frame_local = noisy_clips.shape[1]
    side_len = noisy_clips.shape[2]
    block_shape = noisy_clips.shape[1:]
    tick_count = clip_count + sections - 1
    half_sections = sections // 2
    is_up = segment_id >= half_sections
    store_depth = max(half_sections - 1, 1)
    side_store = jnp.zeros((store_depth,) + block_shape, jnp.bfloat16)
    out_store = jnp.zeros(noisy_clips.shape, jnp.bfloat16)
    prev_out = jnp.zeros(block_shape, jnp.bfloat16)

    def tick_step(carry, tick_index):
        prev_out, side_store, out_store = carry
        clip_now = tick_index - segment_id
        active = (clip_now >= 0) & (clip_now < clip_count)
        clip_slot = jnp.clip(clip_now, 0, clip_count - 1)
        own_input = lax.dynamic_index_in_dim(noisy_clips, clip_slot, 0, keepdims=False)
        received, side_store = passed_along((prev_out, side_store), "segment", 1)
        entering = jnp.where(segment_id == 0, own_input, received)
        written = (jnp.arange(store_depth) == segment_id - 1) & (segment_id < half_sections)
        side_store = jnp.where(written[:, None, None, None, None], entering[None], side_store)
        stack_slot = jnp.clip(sections - 2 - segment_id, 0, store_depth - 1)
        stored = lax.dynamic_index_in_dim(side_store, stack_slot, 0, keepdims=False)
        skip_feature = jnp.where(segment_id == sections - 1, own_input, stored)
        joined = (
            (entering.astype(jnp.float32) + skip_feature.astype(jnp.float32)) * skip_scale
        ).astype(jnp.bfloat16)
        section_in = jnp.where(is_up, joined, entering)
        activated = lax.cond(
            active,
            lambda: jax.nn.silu(spatial(section_in, first_kernel)).astype(jnp.bfloat16),
            lambda: jnp.zeros(block_shape, jnp.bfloat16),
        )
        extended = extended_2(activated, (("frame", 0),), 1)

        def second_pass():
            branch_sum = spatial(activated, second_kernel) + temporal_mix(
                extended, time_kernel, frame_local
            )
            return (section_in.astype(jnp.float32) + jax.nn.silu(branch_sum)).astype(jnp.bfloat16)

        section_out = lax.cond(active, second_pass, lambda: jnp.zeros(block_shape, jnp.bfloat16))
        finished = (jnp.arange(clip_count) == clip_slot) & active & (segment_id == sections - 1)
        out_store = jnp.where(finished[:, None, None, None, None], section_out[None], out_store)
        return ((section_out, side_store, out_store), None)

    final_carry, unused = lax.scan(
        tick_step, (prev_out, side_store, out_store), jnp.arange(tick_count, dtype=jnp.int32)
    )
    delivered = broadcast(final_carry[2], "segment", sections - 1)
    slab_rows = side_len // sections
    return lax.dynamic_slice_in_dim(delivered, segment_id * slab_rows, slab_rows, 2)


def fused_kernel(
    frames,
    noisy_ref,
    first_ref,
    second_ref,
    time_ref,
    out_ref,
    w_ref,
    xe,
    xa,
    a_send,
    a_recv,
    t_send,
    t_recv,
    e_mine,
    e_recv,
    acc_ref,
    o_full,
    o_take,
    local_sem,
    y_sems,
    ring_sems,
    pair_sems,
    a_sems,
    t_sems,
    e_sems,
    o_sems,
):
    clips, side, lanes = noisy_ref.shape[0], noisy_ref.shape[2], noisy_ref.shape[4]
    half = lanes // 2
    cells = side * side
    depth = first_ref.shape[2]
    taps = first_ref.shape[1] + time_ref.shape[1] + second_ref.shape[1]
    n = frames // 2
    seg = lax.axis_index("segment")
    me = lax.axis_index("frame")
    core, chip = lax.rem(me, 2), me // 2
    peer = 1 - seg
    other = chip * 2 + (1 - core)

    def frame_at(place):
        place = lax.rem(place + 2 * n, n)
        return jnp.where(place < n // 2, 2 * place, 2 * (n - 1 - place) + 1) * 2 + core

    pos = jnp.where(lax.rem(chip, 2) == 0, chip // 2, n - 1 - chip // 2)
    right, left = frame_at(pos + 1), frame_at(pos - 1)
    after, before = lax.rem(me + 1, frames), lax.rem(me + frames - 1, frames)

    barrier = pltpu.get_barrier_semaphore()
    pl.semaphore_signal(barrier, inc=1, device_id=(peer, me), device_id_type=MESH)
    for target in (right, left, other, after, before):
        pl.semaphore_signal(barrier, inc=1, device_id=(seg, target), device_id_type=MESH)
    pl.semaphore_wait(barrier, 6)

    def columns(which):
        return pl.ds(pl.multiple_of(which * half, half), half)

    parts = ((first_ref, 0, 9), (time_ref, 9, 3), (second_ref, 12, 9))
    own_rows = pl.ds(pl.multiple_of(me * depth, depth), depth)

    def local_copy(i):
        ref, start, count = parts[i]
        return pltpu.make_async_copy(
            ref.at[0, :, :, columns(seg)],
            w_ref.at[pl.ds(seg * taps + start, count), own_rows],
            local_sem.at[i],
        )

    def remote(src, dst, sems, index, device):
        return pltpu.make_async_remote_copy(
            src_ref=src,
            dst_ref=dst,
            send_sem=sems.at[(0,) + index],
            recv_sem=sems.at[(1,) + index],
            device_id=device,
            device_id_type=MESH,
        )

    def y_copy(i):
        ref, start, count = parts[i]
        return remote(
            ref.at[0, :, :, columns(peer)],
            w_ref.at[pl.ds(seg * taps + start, count), own_rows],
            y_sems,
            (i,),
            (peer, me),
        )

    for i in range(3):
        y_copy(i).start()
        local_copy(i).start()

    groups = (
        (0, (0,), ((0, 5), (5, 4))),
        (0, (1, 2), ((9, 6), (15, 6))),
        (1, (0,), ((0, 5), (5, 4))),
        (1, (1, 2), ((9, 6), (15, 6))),
    )
    streams = tuple((way, sub) for sub in range(2) for way in range(2))
    mid = depth // 2

    def slab(g, q, step):
        section, _, subs = groups[g]
        way, sub = streams[q]
        start, count = subs[sub]
        owner = frame_at(pos - step if way == 0 else pos + step)
        rows = pl.ds(pl.multiple_of(owner * depth + way * mid, mid), mid)
        return w_ref.at[pl.ds(section * taps + start, count), rows]

    def ring(g, q, step):
        ref = slab(g, q, step)
        return remote(ref, ref, ring_sems, (g, q, step), (seg, right if streams[q][0] == 0 else left))

    def paired(g, q, step):
        ref = slab(g, q, step)
        return remote(ref, ref, pair_sems, (g, q, step), (seg, other))

    every = range(len(streams))

    def begin(g):
        section, needed, _ = groups[g]

        @pl.when(seg == section)
        def _():
            for i in needed:
                local_copy(i).wait()

        @pl.when(seg != section)
        def _():
            for i in needed:
                y_copy(i).wait_recv()

        for q in every:
            ring(g, q, 0).start()
            paired(g, q, 0).start()

    def advance(g, step):
        for q in every:
            ring(g, q, step - 1).wait_recv()

            @pl.when(step < n - 1)
            def _():
                ring(g, q, step).start()

            paired(g, q, step).start()

    def complete(g):
        @pl.loop(0, n)
        def _(step):
            for q in every:
                paired(g, q, step).wait_recv()

    def build(x, clip, value, where):
        width = value.shape[1]
        wide = value.astype(jnp.float32)
        place = lax.broadcasted_iota(jnp.int32, (cells, width), 0) % side
        shifted = (
            jnp.where(place == 0, 0.0, pltpu.roll(wide, 1, 0)).astype(jnp.bfloat16),
            value,
            jnp.where(place == side - 1, 0.0, pltpu.roll(wide, cells - 1, 0)).astype(jnp.bfloat16),
        )
        for dx in range(3):
            x[dx, clip, 1 : side + 1, :, where] = shifted[dx].reshape(side, side, width)

    def spatial_sum(x, clip, base):
        total = None
        for dy in range(3):
            for dx in range(3):
                view = x[dx, clip, dy : dy + side].reshape(cells, lanes)
                term = jnp.dot(
                    view, w_ref[base + 3 * dy + dx], preferred_element_type=jnp.float32
                )
                total = term if total is None else total + term
        return total

    def silu(u):
        return u / (1.0 + jnp.exp(-u))

    def a_copy(s, clip):
        return remote(a_send.at[s, clip], a_recv.at[s, clip], a_sems, (s, clip), (peer, me))

    def e_copy(clip):
        return remote(e_mine.at[clip], e_recv.at[clip], e_sems, (clip,), (peer, me))

    def t_copy(s, way, clip):
        target = after if way == 0 else before
        return remote(
            t_send.at[s, way, clip], t_recv.at[s, way, clip], t_sems, (s, way, clip), (seg, target)
        )

    def first_conv(s, clip):
        total = spatial_sum(xe, clip, s * taps)
        a_send[s, clip] = silu(total).astype(jnp.bfloat16)
        a_copy(s, clip).start()

    def take_active(s, clip):
        a_copy(s, clip).wait_recv()
        build(xa, clip, a_send[s, clip], columns(seg))
        build(xa, clip, a_recv[s, clip], columns(peer))

    sends_on = (me < frames - 1, me > 0)
    takes_on = (me > 0, me < frames - 1)

    def mixed(s, clip, k):
        view = xa[1, clip, 1 : side + 1].reshape(cells, lanes)
        return jnp.dot(view, w_ref[s * taps + 9 + k], preferred_element_type=jnp.float32)

    def send_terms(s, clip):
        for way, k in ((0, 0), (1, 2)):
            t_send[s, way, clip] = mixed(s, clip, k).astype(jnp.bfloat16)

            @pl.when(sends_on[way])
            def _():
                t_copy(s, way, clip).start()

    def second_conv(s, clip):
        acc_ref[clip] = spatial_sum(xa, clip, s * taps + 12) + mixed(s, clip, 1)

    def finished(s, clip):
        for way in range(2):

            @pl.when(takes_on[way])
            def _():
                t_copy(s, way, clip).wait_recv()
                acc_ref[clip] = acc_ref[clip] + t_recv[s, way, clip].astype(jnp.float32)

        return silu(acc_ref[clip])

    def end_first(clip):
        own = noisy_ref[clip, 0, :, :, columns(seg)].reshape(cells, half).astype(jnp.float32)
        out = (own + finished(0, clip)).astype(jnp.bfloat16)
        e_mine[clip] = ((out.astype(jnp.float32) + own) * skip_scale).astype(jnp.bfloat16)
        e_copy(clip).start()

    def take_entering(clip):
        e_copy(clip).wait_recv()
        build(xe, clip, e_mine[clip], columns(seg))
        build(xe, clip, e_recv[clip], columns(peer))

    def end_second(clip):
        out = (e_mine[clip].astype(jnp.float32) + finished(1, clip)).astype(jnp.bfloat16)
        o_full[clip] = out.reshape(side, side, half)
        o_send(clip).start()

    def o_send(clip):
        slab_rows = side // 2
        return remote(
            o_full.at[clip, pl.ds(peer * slab_rows, slab_rows)],
            o_take.at[clip],
            o_sems,
            (clip,),
            (peer, me),
        )

    def staged(steps, plan):
        for offset, work in plan:

            @pl.when((steps >= offset) & (steps < offset + clips))
            def _():
                work(steps - offset)

    def overlap(g, plan):
        last = max([n] + [offset + clips for offset, _ in plan])

        @pl.loop(1, last)
        def _(step):
            @pl.when(step < n)
            def _():
                advance(g, step)

            if g + 1 < len(groups):

                @pl.when(step == n - 2)
                def _():
                    begin(g + 1)

            staged(step, plan)

        complete(g)

    begin(0)
    edge = jnp.zeros((side, lanes), jnp.bfloat16)
    for x in (xe, xa):
        for dx in range(3):

            @pl.loop(0, clips)
            def _(clip):
                x[dx, clip, 0] = edge
                x[dx, clip, side + 1] = edge

    overlap(0, ((1, lambda clip: build(xe, clip, noisy_ref[clip, 0].reshape(cells, lanes), slice(None))),))
    overlap(1, ((1, lambda clip: first_conv(0, clip)), (4, lambda clip: take_active(0, clip))))

    def both(s):
        def work(clip):
            send_terms(s, clip)
            second_conv(s, clip)

        return work

    overlap(2, ((1, both(0)), (4, end_first)))
    overlap(
        3,
        (
            (1, take_entering),
            (2, lambda clip: first_conv(1, clip)),
            (4, lambda clip: take_active(1, clip)),
        ),
    )

    @pl.loop(0, clips)
    def _(clip):
        send_terms(1, clip)

    @pl.loop(0, clips)
    def _(clip):
        second_conv(1, clip)
        end_second(clip)

    slab_rows = side // 2

    @pl.loop(0, clips)
    def _(clip):
        out_ref[clip, 0, :, :, columns(seg)] = o_full[clip, pl.ds(seg * slab_rows, slab_rows)]
        o_send(clip).wait_recv()
        out_ref[clip, 0, :, :, columns(peer)] = o_take[clip]
        o_send(clip).wait_send()
        e_copy(clip).wait_send()
        for s in range(2):
            a_copy(s, clip).wait_send()
            for way in range(2):

                @pl.when(sends_on[way])
                def _():
                    t_copy(s, way, clip).wait_send()

    for i in range(3):
        y_copy(i).wait_send()

    @pl.loop(0, n)
    def _(step):
        for g in range(len(groups)):
            for q in every:
                paired(g, q, step).wait_send()

                @pl.when(step < n - 1)
                def _():
                    ring(g, q, step).wait_send()


def on_device(noisy_clips, conv_first, conv_second, temporal):
    sections = lax.axis_size("segment")
    frames = lax.axis_size("frame")
    clips, frame_local, side, _, lanes = noisy_clips.shape
    half = lanes // 2
    cells = side * side
    if sections != 2 or half % 128 or frames % 4 or frames < 8 or frame_local != 1 or side % 16:
        return pipelined(noisy_clips, conv_first, conv_second, temporal)
    n = frames // 2
    dma = pltpu.SemaphoreType.DMA
    vmem = pl.BlockSpec(memory_space=pltpu.VMEM)
    kind = jnp.bfloat16
    return pl.pallas_call(
        functools.partial(fused_kernel, frames),
        out_shape=jax.ShapeDtypeStruct((clips, 1, side // 2, side, lanes), kind),
        in_specs=[vmem] * 4,
        out_specs=vmem,
        scratch_shapes=[
            pltpu.VMEM((42, lanes, half), kind),
            pltpu.VMEM((3, clips, side + 2, side, lanes), kind),
            pltpu.VMEM((3, clips, side + 2, side, lanes), kind),
            pltpu.VMEM((2, clips, cells, half), kind),
            pltpu.VMEM((2, clips, cells, half), kind),
            pltpu.VMEM((2, 2, clips, cells, half), kind),
            pltpu.VMEM((2, 2, clips, cells, half), kind),
            pltpu.VMEM((clips, cells, half), kind),
            pltpu.VMEM((clips, cells, half), kind),
            pltpu.VMEM((clips, cells, half), jnp.float32),
            pltpu.VMEM((clips, side, side, half), kind),
            pltpu.VMEM((clips, side // 2, side, half), kind),
            dma((3,)),
            dma((2, 3)),
            dma((2, 4, 4, n)),
            dma((2, 4, 4, n)),
            dma((2, 2, clips)),
            dma((2, 2, 2, clips)),
            dma((2, clips)),
            dma((2, clips)),
        ],
        compiler_params=pltpu.CompilerParams(
            collective_id=0, has_side_effects=True, vmem_limit_bytes=58 * 1024 * 1024
        ),
    )(noisy_clips, conv_first, conv_second, temporal)


def solution(mesh):
    in_specs = (
        P(None, "frame", None, None, None),
        P("segment", None, "frame", None),
        P("segment", None, "frame", None),
        P("segment", None, "frame", None),
    )
    out_specs = P(None, "frame", "segment", None, None)
    return jax.shard_map(
        on_device, mesh=mesh, in_specs=in_specs, out_specs=out_specs, check_vma=False
    )
```

```python
import functools

import jax
import jax.numpy as jnp
from jax import lax
from jax.experimental import pallas as pl
from jax.experimental.pallas import tpu as pltpu
from jax.sharding import PartitionSpec as P

skip_scale = 0.7071067811865476
MESH = pl.DeviceIdType.MESH


def passed_along(shard, axis, by):
    length = lax.axis_size(axis)
    pairs = [(i, i + by) for i in range(length) if 0 <= i + by < length]
    return lax.ppermute(shard, axis, pairs)


def extended_2(cells, sides, width):
    for axis, dim in sides:
        count = lax.axis_size(axis)
        ends = count - 1
        head = lax.slice_in_dim(cells, 0, width, axis=dim)
        tail = lax.slice_in_dim(cells, cells.shape[dim] - width, cells.shape[dim], axis=dim)
        cells = jnp.concatenate(
            [
                lax.ppermute(tail, axis, [(i, (i + 1) % count) for i in range(ends)]),
                cells,
                lax.ppermute(head, axis, [((i + 1) % count, i) for i in range(ends)]),
            ],
            axis=dim,
        )
    return cells


def broadcast(shard, axis, root):
    mine = lax.axis_index(axis) == root
    return lax.psum(jnp.where(mine, shard, jnp.zeros_like(shard)), axis)


def spatial(field_in, kernel):
    extent = field_in.shape[1]
    channels = field_in.shape[3]
    padded = jnp.pad(field_in, ((0, 0), (1, 1), (1, 1), (0, 0)))
    accumulated = jnp.zeros((field_in.shape[0] * extent * extent, channels), jnp.float32)
    for row_shift in range(3):
        for col_shift in range(3):
            window = padded[
                :, row_shift : row_shift + extent, col_shift : col_shift + extent, :
            ].reshape(-1, channels)
            accumulated = accumulated + jnp.dot(
                window, kernel[3 * row_shift + col_shift], preferred_element_type=jnp.float32
            )
    return accumulated.reshape(field_in.shape)


def temporal_mix(extended, kernel, frame_local):
    channels = extended.shape[3]
    out_shape = (frame_local,) + extended.shape[1:]
    accumulated = jnp.zeros(out_shape, jnp.float32)
    for offset in range(3):
        window = extended[offset : offset + frame_local].reshape(-1, channels)
        accumulated = accumulated + jnp.dot(
            window, kernel[offset], preferred_element_type=jnp.float32
        ).reshape(out_shape)
    return accumulated


def pipelined(noisy_clips, conv_first, conv_second, temporal):
    sections = lax.axis_size("segment")
    segment_id = lax.axis_index("segment")
    first_full, second_full, time_full = (
        lax.all_gather(conv_first, "frame", axis=2, tiled=True),
        lax.all_gather(conv_second, "frame", axis=2, tiled=True),
        lax.all_gather(temporal, "frame", axis=2, tiled=True),
    )
    first_kernel = first_full[0]
    second_kernel = second_full[0]
    time_kernel = time_full[0]
    clip_count = noisy_clips.shape[0]
    frame_local = noisy_clips.shape[1]
    side_len = noisy_clips.shape[2]
    block_shape = noisy_clips.shape[1:]
    tick_count = clip_count + sections - 1
    half_sections = sections // 2
    is_up = segment_id >= half_sections
    store_depth = max(half_sections - 1, 1)
    side_store = jnp.zeros((store_depth,) + block_shape, jnp.bfloat16)
    out_store = jnp.zeros(noisy_clips.shape, jnp.bfloat16)
    prev_out = jnp.zeros(block_shape, jnp.bfloat16)

    def tick_step(carry, tick_index):
        prev_out, side_store, out_store = carry
        clip_now = tick_index - segment_id
        active = (clip_now >= 0) & (clip_now < clip_count)
        clip_slot = jnp.clip(clip_now, 0, clip_count - 1)
        own_input = lax.dynamic_index_in_dim(noisy_clips, clip_slot, 0, keepdims=False)
        received, side_store = passed_along((prev_out, side_store), "segment", 1)
        entering = jnp.where(segment_id == 0, own_input, received)
        written = (jnp.arange(store_depth) == segment_id - 1) & (segment_id < half_sections)
        side_store = jnp.where(written[:, None, None, None, None], entering[None], side_store)
        stack_slot = jnp.clip(sections - 2 - segment_id, 0, store_depth - 1)
        stored = lax.dynamic_index_in_dim(side_store, stack_slot, 0, keepdims=False)
        skip_feature = jnp.where(segment_id == sections - 1, own_input, stored)
        joined = (
            (entering.astype(jnp.float32) + skip_feature.astype(jnp.float32)) * skip_scale
        ).astype(jnp.bfloat16)
        section_in = jnp.where(is_up, joined, entering)
        activated = lax.cond(
            active,
            lambda: jax.nn.silu(spatial(section_in, first_kernel)).astype(jnp.bfloat16),
            lambda: jnp.zeros(block_shape, jnp.bfloat16),
        )
        extended = extended_2(activated, (("frame", 0),), 1)

        def second_pass():
            branch_sum = spatial(activated, second_kernel) + temporal_mix(
                extended, time_kernel, frame_local
            )
            return (section_in.astype(jnp.float32) + jax.nn.silu(branch_sum)).astype(jnp.bfloat16)

        section_out = lax.cond(active, second_pass, lambda: jnp.zeros(block_shape, jnp.bfloat16))
        finished = (jnp.arange(clip_count) == clip_slot) & active & (segment_id == sections - 1)
        out_store = jnp.where(finished[:, None, None, None, None], section_out[None], out_store)
        return ((section_out, side_store, out_store), None)

    final_carry, unused = lax.scan(
        tick_step, (prev_out, side_store, out_store), jnp.arange(tick_count, dtype=jnp.int32)
    )
    delivered = broadcast(final_carry[2], "segment", sections - 1)
    slab_rows = side_len // sections
    return lax.dynamic_slice_in_dim(delivered, segment_id * slab_rows, slab_rows, 2)


def fused_kernel(
    frames,
    noisy_ref,
    first_ref,
    second_ref,
    time_ref,
    out_ref,
    w_ref,
    xe,
    xa,
    a_send,
    a_recv,
    t_send,
    t_recv,
    e_mine,
    e_recv,
    acc_ref,
    o_full,
    o_take,
    local_sem,
    y_sems,
    ring_sems,
    pair_sems,
    a_sems,
    t_sems,
    e_sems,
    o_sems,
):
    clips, side, lanes = noisy_ref.shape[0], noisy_ref.shape[2], noisy_ref.shape[4]
    half = lanes // 2
    cells = side * side
    depth = first_ref.shape[2]
    taps = first_ref.shape[1] + time_ref.shape[1] + second_ref.shape[1]
    n = frames // 2
    seg = lax.axis_index("segment")
    me = lax.axis_index("frame")
    core, chip = lax.rem(me, 2), me // 2
    peer = 1 - seg
    other = chip * 2 + (1 - core)

    def frame_at(place):
        place = lax.rem(place + 2 * n, n)
        return jnp.where(place < n // 2, 2 * place, 2 * (n - 1 - place) + 1) * 2 + core

    pos = jnp.where(lax.rem(chip, 2) == 0, chip // 2, n - 1 - chip // 2)
    right, left = frame_at(pos + 1), frame_at(pos - 1)
    after, before = lax.rem(me + 1, frames), lax.rem(me + frames - 1, frames)

    barrier = pltpu.get_barrier_semaphore()
    pl.semaphore_signal(barrier, inc=1, device_id=(peer, me), device_id_type=MESH)
    for target in (right, left, other, after, before):
        pl.semaphore_signal(barrier, inc=1, device_id=(seg, target), device_id_type=MESH)
    pl.semaphore_wait(barrier, 6)

    def columns(which):
        return pl.ds(pl.multiple_of(which * half, half), half)

    parts = ((first_ref, 0, 9), (time_ref, 9, 3), (second_ref, 12, 9))
    own_rows = pl.ds(pl.multiple_of(me * depth, depth), depth)

    def local_copy(i):
        ref, start, count = parts[i]
        return pltpu.make_async_copy(
            ref.at[0, :, :, columns(seg)],
            w_ref.at[pl.ds(seg * taps + start, count), own_rows],
            local_sem.at[i],
        )

    def remote(src, dst, sems, index, device):
        return pltpu.make_async_remote_copy(
            src_ref=src,
            dst_ref=dst,
            send_sem=sems.at[(0,) + index],
            recv_sem=sems.at[(1,) + index],
            device_id=device,
            device_id_type=MESH,
        )

    def y_copy(i):
        ref, start, count = parts[i]
        return remote(
            ref.at[0, :, :, columns(peer)],
            w_ref.at[pl.ds(seg * taps + start, count), own_rows],
            y_sems,
            (i,),
            (peer, me),
        )

    for i in range(3):
        y_copy(i).start()
        local_copy(i).start()

    groups = (
        (0, (0,), ((0, 5), (5, 4))),
        (0, (1, 2), ((9, 6), (15, 6))),
        (1, (0,), ((0, 5), (5, 4))),
        (1, (1, 2), ((9, 6), (15, 6))),
    )
    streams = tuple((way, sub) for sub in range(2) for way in range(2))
    mid = depth // 2

    def slab(g, q, step):
        section, _, subs = groups[g]
        way, sub = streams[q]
        start, count = subs[sub]
        owner = frame_at(pos - step if way == 0 else pos + step)
        rows = pl.ds(pl.multiple_of(owner * depth + way * mid, mid), mid)
        return w_ref.at[pl.ds(section * taps + start, count), rows]

    def ring(g, q, step):
        ref = slab(g, q, step)
        return remote(ref, ref, ring_sems, (g, q, step), (seg, right if streams[q][0] == 0 else left))

    def paired(g, q, step):
        ref = slab(g, q, step)
        return remote(ref, ref, pair_sems, (g, q, step), (seg, other))

    every = range(len(streams))

    def begin(g):
        section, needed, _ = groups[g]

        @pl.when(seg == section)
        def _():
            for i in needed:
                local_copy(i).wait()

        @pl.when(seg != section)
        def _():
            for i in needed:
                y_copy(i).wait_recv()

        for q in every:
            ring(g, q, 0).start()
            paired(g, q, 0).start()

    def advance(g, step):
        for q in every:
            ring(g, q, step - 1).wait_recv()

            @pl.when(step < n - 1)
            def _():
                ring(g, q, step).start()

            paired(g, q, step).start()

    def complete(g):
        @pl.loop(0, n)
        def _(step):
            for q in every:
                paired(g, q, step).wait_recv()

    def build(x, clip, value, where):
        width = value.shape[1]
        wide = value.astype(jnp.float32)
        place = lax.broadcasted_iota(jnp.int32, (cells, width), 0) % side
        shifted = (
            jnp.where(place == 0, 0.0, pltpu.roll(wide, 1, 0)).astype(jnp.bfloat16),
            value,
            jnp.where(place == side - 1, 0.0, pltpu.roll(wide, cells - 1, 0)).astype(jnp.bfloat16),
        )
        for dx in range(3):
            x[dx, clip, 1 : side + 1, :, where] = shifted[dx].reshape(side, side, width)

    def spatial_sum(x, clip, base):
        total = None
        for dy in range(3):
            for dx in range(3):
                view = x[dx, clip, dy : dy + side].reshape(cells, lanes)
                term = jnp.dot(
                    view, w_ref[base + 3 * dy + dx], preferred_element_type=jnp.float32
                )
                total = term if total is None else total + term
        return total

    def silu(u):
        return u / (1.0 + jnp.exp(-u))

    def a_copy(s, clip):
        return remote(a_send.at[s, clip], a_recv.at[s, clip], a_sems, (s, clip), (peer, me))

    def e_copy(clip):
        return remote(e_mine.at[clip], e_recv.at[clip], e_sems, (clip,), (peer, me))

    def t_copy(s, way, clip):
        target = after if way == 0 else before
        return remote(
            t_send.at[s, way, clip], t_recv.at[s, way, clip], t_sems, (s, way, clip), (seg, target)
        )

    def first_conv(s, clip):
        total = spatial_sum(xe, clip, s * taps)
        a_send[s, clip] = silu(total).astype(jnp.bfloat16)
        a_copy(s, clip).start()

    def take_active(s, clip):
        a_copy(s, clip).wait_recv()
        build(xa, clip, a_send[s, clip], columns(seg))
        build(xa, clip, a_recv[s, clip], columns(peer))

    sends_on = (me < frames - 1, me > 0)
    takes_on = (me > 0, me < frames - 1)

    def mixed(s, clip, k):
        view = xa[1, clip, 1 : side + 1].reshape(cells, lanes)
        return jnp.dot(view, w_ref[s * taps + 9 + k], preferred_element_type=jnp.float32)

    def send_terms(s, clip):
        for way, k in ((0, 0), (1, 2)):
            t_send[s, way, clip] = mixed(s, clip, k).astype(jnp.bfloat16)

            @pl.when(sends_on[way])
            def _():
                t_copy(s, way, clip).start()

    def second_conv(s, clip):
        acc_ref[clip] = spatial_sum(xa, clip, s * taps + 12) + mixed(s, clip, 1)

    def finished(s, clip):
        for way in range(2):

            @pl.when(takes_on[way])
            def _():
                t_copy(s, way, clip).wait_recv()
                acc_ref[clip] = acc_ref[clip] + t_recv[s, way, clip].astype(jnp.float32)

        return silu(acc_ref[clip])

    def end_first(clip):
        own = noisy_ref[clip, 0, :, :, columns(seg)].reshape(cells, half).astype(jnp.float32)
        out = (own + finished(0, clip)).astype(jnp.bfloat16)
        e_mine[clip] = ((out.astype(jnp.float32) + own) * skip_scale).astype(jnp.bfloat16)
        e_copy(clip).start()

    def take_entering(clip):
        e_copy(clip).wait_recv()
        build(xe, clip, e_mine[clip], columns(seg))
        build(xe, clip, e_recv[clip], columns(peer))

    def end_second(clip):
        out = (e_mine[clip].astype(jnp.float32) + finished(1, clip)).astype(jnp.bfloat16)
        o_full[clip] = out.reshape(side, side, half)
        o_send(clip).start()

    def o_send(clip):
        slab_rows = side // 2
        return remote(
            o_full.at[clip, pl.ds(peer * slab_rows, slab_rows)],
            o_take.at[clip],
            o_sems,
            (clip,),
            (peer, me),
        )

    def staged(steps, plan):
        for offset, work in plan:

            @pl.when((steps >= offset) & (steps < offset + clips))
            def _():
                work(steps - offset)

    edge = jnp.zeros((side, lanes), jnp.bfloat16)
    for x in (xe, xa):
        for dx in range(3):

            @pl.loop(0, clips)
            def _(clip):
                x[dx, clip, 0] = edge
                x[dx, clip, side + 1] = edge

    def both(s):
        def work(clip):
            send_terms(s, clip)
            second_conv(s, clip)

        return work

    skew = n // 2 - 1
    ready = [g * skew + n for g in range(len(groups))]
    start_terms = max(ready[1], ready[0] + 4)
    start_next = max(ready[2], start_terms + 5)
    plan = (
        (0, lambda clip: build(xe, clip, noisy_ref[clip, 0].reshape(cells, lanes), slice(None))),
        (ready[0], lambda clip: first_conv(0, clip)),
        (start_terms - 1, lambda clip: take_active(0, clip)),
        (start_terms, both(0)),
        (start_terms + 2, end_first),
        (start_next - 1, take_entering),
        (start_next, lambda clip: first_conv(1, clip)),
        (start_next + 3, lambda clip: take_active(1, clip)),
    )
    last = max([ready[-1] + 1] + [offset + clips for offset, _ in plan])

    @pl.loop(0, last)
    def _(step):
        for g in range(len(groups)):

            @pl.when((step > g * skew) & (step < ready[g]))
            def _():
                advance(g, step - g * skew)

            @pl.when(step == g * skew)
            def _():
                begin(g)

            @pl.when(step == ready[g])
            def _():
                complete(g)

        staged(step, plan)

    @pl.loop(0, clips)
    def _(clip):
        send_terms(1, clip)

    @pl.loop(0, clips)
    def _(clip):
        second_conv(1, clip)
        end_second(clip)

    slab_rows = side // 2

    @pl.loop(0, clips)
    def _(clip):
        out_ref[clip, 0, :, :, columns(seg)] = o_full[clip, pl.ds(seg * slab_rows, slab_rows)]
        o_send(clip).wait_recv()
        out_ref[clip, 0, :, :, columns(peer)] = o_take[clip]
        o_send(clip).wait_send()
        e_copy(clip).wait_send()
        for s in range(2):
            a_copy(s, clip).wait_send()
            for way in range(2):

                @pl.when(sends_on[way])
                def _():
                    t_copy(s, way, clip).wait_send()

    for i in range(3):
        y_copy(i).wait_send()

    @pl.loop(0, n)
    def _(step):
        for g in range(len(groups)):
            for q in every:
                paired(g, q, step).wait_send()

                @pl.when(step < n - 1)
                def _():
                    ring(g, q, step).wait_send()


def on_device(noisy_clips, conv_first, conv_second, temporal):
    sections = lax.axis_size("segment")
    frames = lax.axis_size("frame")
    clips, frame_local, side, _, lanes = noisy_clips.shape
    half = lanes // 2
    cells = side * side
    if sections != 2 or half % 128 or frames % 4 or frames < 8 or frame_local != 1 or side % 16:
        return pipelined(noisy_clips, conv_first, conv_second, temporal)
    n = frames // 2
    dma = pltpu.SemaphoreType.DMA
    vmem = pl.BlockSpec(memory_space=pltpu.VMEM)
    kind = jnp.bfloat16
    return pl.pallas_call(
        functools.partial(fused_kernel, frames),
        out_shape=jax.ShapeDtypeStruct((clips, 1, side // 2, side, lanes), kind),
        in_specs=[vmem] * 4,
        out_specs=vmem,
        scratch_shapes=[
            pltpu.VMEM((42, lanes, half), kind),
            pltpu.VMEM((3, clips, side + 2, side, lanes), kind),
            pltpu.VMEM((3, clips, side + 2, side, lanes), kind),
            pltpu.VMEM((2, clips, cells, half), kind),
            pltpu.VMEM((2, clips, cells, half), kind),
            pltpu.VMEM((2, 2, clips, cells, half), kind),
            pltpu.VMEM((2, 2, clips, cells, half), kind),
            pltpu.VMEM((clips, cells, half), kind),
            pltpu.VMEM((clips, cells, half), kind),
            pltpu.VMEM((clips, cells, half), jnp.float32),
            pltpu.VMEM((clips, side, side, half), kind),
            pltpu.VMEM((clips, side // 2, side, half), kind),
            dma((3,)),
            dma((2, 3)),
            dma((2, 4, 4, n)),
            dma((2, 4, 4, n)),
            dma((2, 2, clips)),
            dma((2, 2, 2, clips)),
            dma((2, clips)),
            dma((2, clips)),
        ],
        compiler_params=pltpu.CompilerParams(
            collective_id=0, has_side_effects=True, vmem_limit_bytes=58 * 1024 * 1024
        ),
    )(noisy_clips, conv_first, conv_second, temporal)


def solution(mesh):
    in_specs = (
        P(None, "frame", None, None, None),
        P("segment", None, "frame", None),
        P("segment", None, "frame", None),
        P("segment", None, "frame", None),
    )
    out_specs = P(None, "frame", "segment", None, None)
    return jax.shard_map(
        on_device, mesh=mesh, in_specs=in_specs, out_specs=out_specs, check_vma=False
    )
```
